32 devices in a mesh: grp: 4 (over y, x), row: 2 (over core), col: 4 (over z).
Axes of the slice: x: 2, y: 2, z: 4, core: 2. Of those that a mesh axis runs over, the one named last changes fastest.
Arguments:
- layer_windows: bfloat16 [4, 768, 16384], P(None, ('row', 'grp', 'col')), may hold values from -0.046875 to 0.046875
- sketches: bfloat16 [4, 16384, 128], P(None, 'col'), may hold values from -6 to 6
- group_of: int32 [4], replicated, may hold values from 0 to 3, each once
Outputs:
- basis: float32 [4, 768, 128], P('grp', ('row', 'col'))
- projection: float32 [4, 128, 16384], P('grp', None, 'col')
The draws below stay inside these ranges and needn't reach their ends.
Inputs may be any that keep to these rules, and one draw needn't show every extreme that they name: `group_of`: each group audits exactly one matrix.
All inputs are finite; a program needn't handle non-finite values.
Results may differ from the reference program's by a relative error of at most 0.013.
Values may be sent and summed in bfloat16 or wider, within the bound.
A program may use at most 64 MiB of HBM per device.

```python
import math
import jax
import jax.numpy as jnp
from jax import lax

COLS = 16384
RANK = 128
MATS = 4
ROWS = 768


def block_levels(stream_key, shape, split, smallest, high):
    def one(position, parts):
        heights = jax.random.uniform(jax.random.fold_in(jax.random.fold_in(stream_key, 6), position), (parts,), jnp.float32, smallest / len(split), high / len(split))
        return jnp.repeat(jnp.exp(heights), shape[position] // parts).reshape((-1,) + (1,) * (len(shape) - position - 1))

    factor_of = one(*split[0])
    for cut in split[1:]:
        factor_of = factor_of * one(*cut)
    return factor_of


def normal_values(key, dims, spread, reach, pieces=(), kind=jnp.bfloat16):
    array = spread * jax.random.normal(key, dims, jnp.float32)
    if pieces:
        array = array * block_levels(key, dims, pieces, -0.22, 0.18)
    return jnp.clip(array, -reach, reach).astype(kind)


def setup_inputs(seed: int = 0) -> dict:
    arg_keys = jax.random.split(jax.random.key(seed), 4)
    layer_windows = normal_values(arg_keys[0], (MATS, ROWS, COLS), COLS ** -0.5, 0.046875, ((1, 32),))
    sketches = normal_values(arg_keys[1], (MATS, COLS, RANK), 1.0, 6.0, ((1, 4),))
    group_of = jax.random.permutation(arg_keys[2], MATS).astype(jnp.int32)
    return dict(layer_windows=layer_windows, sketches=sketches, group_of=group_of)


def right_solve(lower, power):
    return lax.linalg.triangular_solve(lower, power, left_side=False, lower=True, transpose_a=True)

def reference(layer_windows, sketches, group_of):
    slots = jnp.arange(MATS, dtype=jnp.int32)
    matched = (group_of[None, :] == slots[:, None]).astype(jnp.int32)
    owner_of = lax.optimization_barrier(jnp.sum(matched * slots[None, :], axis=1)).astype(jnp.int32)
    bases = []
    projections = []
    for slot in range(MATS):
        mine = owner_of[slot]
        matrix = lax.dynamic_index_in_dim(layer_windows, mine, 0, keepdims=False)
        omega = lax.dynamic_index_in_dim(sketches, mine, 0, keepdims=False)
        sketched = jnp.dot(matrix.astype(jnp.float32), omega.astype(jnp.float32), preferred_element_type=jnp.float32).astype(jnp.bfloat16)
        back = jnp.dot(matrix.T.astype(jnp.float32), sketched.astype(jnp.float32), preferred_element_type=jnp.float32).astype(jnp.bfloat16)
        power = jnp.dot(matrix.astype(jnp.float32), back.astype(jnp.float32), preferred_element_type=jnp.float32)
        gram = jnp.dot(power.T, power, precision=lax.Precision.HIGHEST)
        lower = jnp.linalg.cholesky(gram)
        ortho = right_solve(lower, power) * math.sqrt(ROWS)
        ortho_low = ortho.astype(jnp.bfloat16)
        proj = jnp.dot(ortho_low.T.astype(jnp.float32), matrix.astype(jnp.float32), preferred_element_type=jnp.float32) * math.sqrt(COLS / ROWS)
        bases.append(ortho)
        projections.append(proj)
    return (jnp.stack(bases), jnp.stack(projections))
```

```python
import functools
import math

import jax
import jax.numpy as jnp
from jax import lax
from jax.experimental import pallas as pl
from jax.experimental.pallas import tpu as pltpu
from jax.sharding import PartitionSpec as P

MESH = pl.DeviceIdType.MESH
F32 = jnp.float32
BF16 = jnp.bfloat16


def across(left, right):
    return lax.dot_general(
        left, right, (((0,), (0,)), ((), ())), preferred_element_type=jnp.float32
    )


def right_solve(lower, power):
    return lax.linalg.triangular_solve(lower, power, left_side=False, lower=True, transpose_a=True)


def owners(group_of):
    count = group_of.shape[0]
    slots = jnp.arange(count, dtype=jnp.int32)
    matched = (group_of[None, :] == slots[:, None]).astype(jnp.int32)
    return jnp.sum(matched * slots[None, :], axis=1)


def per_device(layer_windows, sketches, group_of):
    owner_of = owners(group_of)
    ordered = jnp.take(layer_windows, owner_of, axis=0)
    block = lax.all_to_all(
        lax.all_to_all(ordered, "col", split_axis=2, concat_axis=1, tiled=True),
        "grp",
        split_axis=0,
        concat_axis=1,
        tiled=True,
    )[0]
    mine = owner_of[lax.axis_index("grp")]
    omega = lax.dynamic_index_in_dim(sketches, mine, 0, keepdims=False)
    total_rows = block.shape[0] * lax.axis_size("row")
    total_cols = block.shape[1] * lax.axis_size("col")
    share = block.shape[0] // lax.axis_size("col")

    def summed_rows(right):
        return lax.psum(jnp.dot(block, right, preferred_element_type=jnp.float32), "col")

    sketched = summed_rows(omega).astype(jnp.bfloat16)
    back = lax.psum(across(block, sketched).astype(jnp.bfloat16), "row")
    power = summed_rows(back)
    gram = lax.psum(
        jnp.dot(power.T, power, precision=lax.Precision.HIGHEST).astype(jnp.bfloat16), "row"
    ).astype(jnp.float32)
    lower = jnp.linalg.cholesky(gram)
    ortho = right_solve(lower, power) * math.sqrt(total_rows)
    basis_share = lax.dynamic_slice_in_dim(ortho, lax.axis_index("col") * share, share, 0)
    ortho_low = ortho.astype(jnp.bfloat16)
    projected = lax.psum(across(ortho_low, block).astype(jnp.bfloat16), "row").astype(
        jnp.float32
    ) * math.sqrt(total_cols / total_rows)
    return (basis_share[None], projected[None])


def range_kernel(groups, zs, chunks, ordered, omega, block, power, gram,
                 part1, part2, rs1, rs2, sk, bt, bt_in, back, gpart, g_in,
                 a_send, a_recv, own_sem, s1_send, s1_recv, g1_send, g1_recv,
                 b_send, b_recv, s2_send, s2_recv, g2_send, g2_recv, x_send, x_recv):
    g, r, c = lax.axis_index("grp"), lax.axis_index("row"), lax.axis_index("col")
    height = ordered.shape[1]
    wide = block.shape[1]
    share = block.shape[0] // zs
    other = (g, 1 - r, c)

    def partner(dz):
        if zs != 4 or dz == 2:
            return lax.rem(c + dz, zs)
        return (c, c + 1 - 2 * lax.rem(c, 2), None, 3 - c)[dz]

    order = (2, 3, 1) if zs == 4 else tuple(range(1, zs))

    barrier = pltpu.get_barrier_semaphore()
    for dz in range(zs):
        for dg in range(groups):
            if dz or dg:
                to = (lax.rem(g + dg, groups), r, partner(dz))
                pl.semaphore_signal(barrier, inc=1, device_id=to, device_id_type=MESH)
    pl.semaphore_signal(barrier, inc=1, device_id=other, device_id_type=MESH)
    pl.semaphore_wait(barrier, groups * zs)

    def spot(gi, ci):
        return block.at[pl.ds(pl.multiple_of((gi * zs + ci) * height, 8), height), :]

    def cut(gi, ci):
        return ordered.at[gi, :, pl.ds(pl.multiple_of(ci * wide, 128), wide)]

    sends = []
    for dz in order + (0,):
        for dg in range(groups):
            tg, tc = lax.rem(g + dg, groups), partner(dz)
            if dz or dg:
                copy = pltpu.make_async_remote_copy(
                    src_ref=cut(tg, tc), dst_ref=spot(g, c),
                    send_sem=a_send.at[dz * groups + dg], recv_sem=a_recv.at[dz * groups + dg],
                    device_id=(tg, r, tc), device_id_type=MESH)
                copy.start()
                sends.append(copy)
    own = pltpu.make_async_copy(cut(g, c), spot(g, c), own_sem)
    own.start()
    own.wait()
    for copy in sends:
        copy.wait()

    def rows(k):
        return pl.ds(pl.multiple_of(k * share, 16), share)

    def scatter(compute, part, rs, send_sem, recv_sem):
        copies = []
        for dz in order:
            k = partner(dz)
            part[dz] = compute(block[rows(k), :])
            copy = pltpu.make_async_remote_copy(
                src_ref=part.at[dz], dst_ref=rs.at[dz],
                send_sem=send_sem.at[dz], recv_sem=recv_sem.at[dz],
                device_id=(g, r, k), device_id_type=MESH)
            copy.start()
            copies.append(copy)
        total = compute(block[rows(c), :])
        for copy in copies:
            copy.wait()
        for dz in range(1, zs):
            total = total + rs[dz]
        return total

    def gather(ref, send_sem, recv_sem):
        copies = []
        for dz in order:
            copy = pltpu.make_async_remote_copy(
                src_ref=ref.at[rows(c), :], dst_ref=ref.at[rows(c), :],
                send_sem=send_sem.at[dz], recv_sem=recv_sem.at[dz],
                device_id=(g, r, partner(dz)), device_id_type=MESH)
            copy.start()
            copies.append(copy)
        for copy in copies:
            copy.wait()

    sk[rows(c), :] = scatter(
        lambda a: jnp.dot(a, omega[...], preferred_element_type=F32),
        part1, rs1, s1_send, s1_recv).astype(BF16)
    gather(sk, g1_send, g1_recv)

    turned = sk[...].astype(F32).T.astype(BF16)
    step = wide // chunks
    copies = []
    for i in range(chunks):
        bt[i] = jnp.dot(turned, block[:, i * step:(i + 1) * step],
                        preferred_element_type=F32).astype(BF16)
        copy = pltpu.make_async_remote_copy(
            src_ref=bt.at[i], dst_ref=bt_in.at[i], send_sem=b_send.at[i], recv_sem=b_recv.at[i],
            device_id=other, device_id_type=MESH)
        copy.start()
        copies.append(copy)
    for i in range(chunks):
        copies[i].wait()
        back[:, i * step:(i + 1) * step] = (bt[i].astype(F32) + bt_in[i].astype(F32)).astype(BF16)

    power[rows(c), :] = scatter(
        lambda a: lax.dot_general(a, back[...], (((1,), (1,)), ((), ())),
                                  preferred_element_type=F32),
        part2, rs2, s2_send, s2_recv)
    gather(power, g2_send, g2_recv)

    whole = power[...]
    gpart[...] = jnp.dot(whole.T, whole, precision=lax.Precision.HIGHEST,
                         preferred_element_type=F32)
    copy = pltpu.make_async_remote_copy(
        src_ref=gpart, dst_ref=g_in, send_sem=x_send, recv_sem=x_recv,
        device_id=other, device_id_type=MESH)
    copy.start()
    copy.wait()
    gram[...] = gpart[...] + g_in[...]


def project_kernel(chunks, turned, block, out, mine, theirs, send_sem, recv_sem):
    other = (lax.axis_index("grp"), 1 - lax.axis_index("row"), lax.axis_index("col"))
    barrier = pltpu.get_barrier_semaphore()
    pl.semaphore_signal(barrier, inc=1, device_id=other, device_id_type=MESH)
    pl.semaphore_wait(barrier, 1)
    step = block.shape[1] // chunks
    copies = []
    for i in range(chunks):
        mine[i] = jnp.dot(turned[...], block[:, i * step:(i + 1) * step],
                          preferred_element_type=F32).astype(BF16)
        copy = pltpu.make_async_remote_copy(
            src_ref=mine.at[i], dst_ref=theirs.at[i],
            send_sem=send_sem.at[i], recv_sem=recv_sem.at[i],
            device_id=other, device_id_type=MESH)
        copy.start()
        copies.append(copy)
    for i in range(chunks):
        copies[i].wait()
        out[:, i * step:(i + 1) * step] = mine[i].astype(F32) + theirs[i].astype(F32)


def fused_device(groups, zs, layer_windows, sketches, group_of):
    owner_of = owners(group_of)
    count, height, total_cols = layer_windows.shape
    rank = sketches.shape[2]
    wide = total_cols // zs
    deep = height * groups * zs
    share = deep // zs
    total_rows = deep * 2
    chunks = 4
    step = wide // chunks
    ordered = layer_windows.at[owner_of].get(mode="promise_in_bounds", unique_indices=True)
    mine = owner_of[lax.axis_index("grp")]
    omega = lax.dynamic_index_in_dim(sketches, mine, 0, keepdims=False)
    vmem = pl.BlockSpec(memory_space=pltpu.VMEM)
    dma = pltpu.SemaphoreType.DMA
    block, power, gram = pl.pallas_call(
        functools.partial(range_kernel, groups, zs, chunks),
        out_shape=(
            jax.ShapeDtypeStruct((deep, wide), BF16),
            jax.ShapeDtypeStruct((deep, rank), F32),
            jax.ShapeDtypeStruct((rank, rank), F32),
        ),
        in_specs=[pl.BlockSpec(memory_space=pl.ANY), vmem],
        out_specs=(vmem, vmem, vmem),
        scratch_shapes=[
            pltpu.VMEM((zs, share, rank), F32),
            pltpu.VMEM((zs, share, rank), F32),
            pltpu.VMEM((zs, share, rank), F32),
            pltpu.VMEM((zs, share, rank), F32),
            pltpu.VMEM((deep, rank), BF16),
            pltpu.VMEM((chunks, rank, step), BF16),
            pltpu.VMEM((chunks, rank, step), BF16),
            pltpu.VMEM((rank, wide), BF16),
            pltpu.VMEM((rank, rank), F32),
            pltpu.VMEM((rank, rank), F32),
            dma((zs * groups,)), dma((zs * groups,)), dma,
            dma((zs,)), dma((zs,)), dma((zs,)), dma((zs,)),
            dma((chunks,)), dma((chunks,)),
            dma((zs,)), dma((zs,)), dma((zs,)), dma((zs,)),
            dma, dma,
        ],
        compiler_params=pltpu.CompilerParams(collective_id=0, has_side_effects=True),
        name="range_finder",
    )(ordered, omega)
    lower = jnp.linalg.cholesky(gram)
    ortho = right_solve(lower, power) * math.sqrt(total_rows)
    basis_share = lax.dynamic_slice_in_dim(ortho, lax.axis_index("col") * share, share, 0)
    turned = ortho.astype(BF16).T
    projected = pl.pallas_call(
        functools.partial(project_kernel, chunks),
        out_shape=jax.ShapeDtypeStruct((rank, wide), F32),
        in_specs=[vmem, vmem],
        out_specs=vmem,
        scratch_shapes=[
            pltpu.VMEM((chunks, rank, step), BF16),
            pltpu.VMEM((chunks, rank, step), BF16),
            dma((chunks,)), dma((chunks,)),
        ],
        compiler_params=pltpu.CompilerParams(collective_id=1, has_side_effects=True),
        name="projector",
    )(turned, block)
    return (basis_share[None], (projected * math.sqrt(total_cols / total_rows))[None])


def solution(mesh):
    in_specs = (P(None, ("row", "grp", "col"), None), P(None, "col", None), P())
    out_specs = (P("grp", ("row", "col"), None), P("grp", None, "col"))
    groups, halves, zs = mesh.shape["grp"], mesh.shape["row"], mesh.shape["col"]

    def body(layer_windows, sketches, group_of):
        height = layer_windows.shape[1]
        fits = halves == 2 and height % 8 == 0 and (height * groups) % 16 == 0
        if fits and groups == layer_windows.shape[0] and layer_windows.shape[2] % (zs * 512) == 0:
            return fused_device(groups, zs, layer_windows, sketches, group_of)
        return per_device(layer_windows, sketches, group_of)

    return jax.shard_map(body, mesh=mesh, in_specs=in_specs, out_specs=out_specs, check_vma=False)
```
